256 devices in a mesh: tm: 16 (over x, y), space: 16 (over z, core).
Axes of the slice: x: 4, y: 4, z: 8, core: 2. Of those that a mesh axis runs over, the one named last changes fastest.
Arguments:
- snapshots: bfloat16 [16, 128, 4, 32, 16, 256], P('tm', None, None, 'space'), may hold values from -8 to 8, as said below
- lat_taps: float32 [4, 32, 5], P(None, 'space'), may hold values from 0.1 to 1
- lon_taps: float32 [4, 32, 5], P(None, 'space'), may hold values from 0.1 to 1
Outputs:
- merged: bfloat16 [16, 128, 4, 32, 1024], P('tm', None, None, 'space')
The draws below stay inside these ranges and needn't reach their ends.
Inputs may be any that keep to these rules, and one draw needn't show every extreme that they name: `snapshots`: Real-valued hourly fields of the window.
All inputs are finite; a program needn't handle non-finite values.
Results may differ from the reference program's by a relative error of at most 0.025.
Values may be sent and summed in bfloat16 or wider, within the bound.
A program may use at most 128 MiB of HBM per device.

```python
import math
from functools import partial
import jax
import jax.numpy as jnp
from jax import lax

SNAP = 128
RANK = 128
VARS = 4
LEVELS = 32
CLAT = 8
CLON = 128
TAPS = 5
LEVEL = 0
ITERS = 4
TIME_BLOCKS = 16


def draw_snapshots(key, part):
    full_shape = (TIME_BLOCKS, SNAP, VARS, LEVELS, 2 * CLAT, 2 * CLON)
    key_base, key_scale, key_order, key_modes = jax.random.split(jax.random.fold_in(key, 11), 4)
    key_freq, key_phase, key_amplitude, key_pattern = jax.random.split(key_modes, 4)
    order_keys = jax.random.split(key_order, TIME_BLOCKS)
    ranks = jax.vmap(lambda single: jax.random.permutation(single, SNAP))(order_keys)
    loud = (ranks < SNAP // 2).reshape(TIME_BLOCKS, SNAP, 1, 1, 1, 1)
    mode_count = 16
    pattern_keys = jax.random.split(key_pattern, mode_count)
    base_field = jax.random.truncated_normal(key_base, -4.0, 4.0, full_shape, jnp.float32)
    pick = jax.random.uniform(key_scale, (TIME_BLOCKS, SNAP, 1, 1, 1, 1), jnp.float32, 0.0, math.log(2.0))
    column_scale = jnp.where(loud, 2.0, 0.5) * jnp.exp(pick)
    period_low = 24.0
    period_high = 4.0 * SNAP
    frequencies = jnp.exp(jax.random.uniform(key_freq, (mode_count,), jnp.float32, math.log(2.0 * math.pi / period_high), math.log(2.0 * math.pi / period_low)))
    phases = jax.random.uniform(key_phase, (mode_count, LEVELS), jnp.float32, 0.0, 2.0 * math.pi)
    amplitudes = jax.random.uniform(key_amplitude, (mode_count, LEVELS), jnp.float32, 0.5, 1.5)
    time_index = (jnp.arange(TIME_BLOCKS)[:, None] * SNAP + jnp.arange(SNAP)[None, :]).astype(jnp.float32).reshape(TIME_BLOCKS, SNAP, 1, 1, 1, 1)
    mode_weight = 0.6 * math.sqrt(2.0 / mode_count)
    total_field = 0.8 * base_field
    for mode_index in range(mode_count):
        pattern = jax.random.truncated_normal(pattern_keys[mode_index], -4.0, 4.0, (1, 1, VARS, 1, 2 * CLAT, 2 * CLON), jnp.float32)
        level_amplitude = amplitudes[mode_index].reshape(1, 1, 1, LEVELS, 1, 1)
        level_phase = phases[mode_index].reshape(1, 1, 1, LEVELS, 1, 1)
        coefficient = mode_weight * level_amplitude * jnp.cos(frequencies[mode_index] * time_index + level_phase)
        total_field = total_field + coefficient * pattern
    level_index = jnp.arange(LEVELS, dtype=jnp.float32) / max(LEVELS - 1, 1)
    level_scale = jnp.exp(level_index * math.log(3.0)).reshape(1, 1, 1, LEVELS, 1, 1)
    scaled = jnp.clip(total_field * column_scale * level_scale * (1.0 / 6.0), -8.0, 8.0)
    return scaled.astype(jnp.bfloat16)


def shard_levels(stream_key, shape, cuts, low, high):
    level = 1.0
    for dim, shards_of in cuts:
        heights = jax.random.uniform(jax.random.fold_in(jax.random.fold_in(stream_key, 6), dim), (shards_of,), jnp.float32, low / len(cuts), high / len(cuts))
        level = level * jnp.repeat(jnp.exp(heights), shape[dim] // shards_of).reshape((-1,) + (1,) * (len(shape) - 1 - dim))
    return level


def setup_inputs(seed: int = 0) -> dict:
    seeds = jax.random.split(jax.random.key(seed), 4)
    return {
        "snapshots": draw_snapshots(jax.random.fold_in(seeds[3], 71), 0),
        "lat_taps": jnp.clip(jnp.exp(math.log(1.0) - 2.3025851 * jax.random.uniform(seeds[1], (VARS, LEVELS, TAPS), jnp.float32) ** shard_levels(seeds[1], (VARS, LEVELS, TAPS), ((1, 16),), -0.2, 0.2)), 0.1, 1.0),
        "lon_taps": jnp.clip(jnp.exp(math.log(1.0) - 2.3025851 * jax.random.uniform(seeds[2], (VARS, LEVELS, TAPS), jnp.float32) ** shard_levels(seeds[2], (VARS, LEVELS, TAPS), ((1, 16),), -0.2, 0.2)), 0.1, 1.0),
    }


def coarsen(fine_field, lat_taps, lon_taps):
    singular_values = fine_field.astype(jnp.float32)
    tap_count = lat_taps.shape[-1]
    reach = tap_count // 2
    coarse_rows = singular_values.shape[-2] // 2
    coarse_cols = singular_values.shape[-1] // 2
    padded = jnp.pad(singular_values, ((0, 0), (0, 0), (0, 0), (0, 0), (reach, reach)))
    across = jnp.zeros(singular_values.shape[:-1] + (coarse_cols,), jnp.float32)
    for offset in range(tap_count):
        weight = lon_taps[:, :, offset][None, :, :, None, None]
        across = across + weight * padded[..., offset:offset + 2 * coarse_cols:2]
    padded = jnp.pad(across, ((0, 0), (0, 0), (0, 0), (reach, reach), (0, 0)))
    result = jnp.zeros(singular_values.shape[:-2] + (coarse_rows, coarse_cols), jnp.float32)
    for offset in range(tap_count):
        weight = lat_taps[:, :, offset][None, :, :, None, None]
        result = result + weight * padded[..., offset:offset + 2 * coarse_rows:2, :]
    return result.astype(jnp.bfloat16).reshape(singular_values.shape[:3] + (coarse_rows * coarse_cols,))

def orthonormal(image_cols):
    product = jnp.dot(image_cols.T, image_cols, precision=lax.Precision.HIGHEST)
    factor = jnp.linalg.cholesky(product)
    return jax.scipy.linalg.solve_triangular(factor, image_cols.T, lower=True).T

def merge_pair(lower_data, upper_data):
    row_total = lower_data.shape[1] * lower_data.shape[2] * lower_data.shape[3]
    stacked = jnp.concatenate([lower_data, upper_data], axis=0).reshape(2 * SNAP, row_total)
    gram_matrix = lax.dot_general(stacked.astype(jnp.float32), stacked.astype(jnp.float32), (((1,), (1,)), ((), ())), preferred_element_type=jnp.float32)
    initial = (jnp.arange(2 * SNAP)[:, None] % RANK == jnp.arange(RANK)[None, :]).astype(jnp.float32)
    basis_cols = initial
    for sweep in range(ITERS):
        image_cols = jnp.dot(gram_matrix, basis_cols, precision=lax.Precision.HIGHEST)
        basis_cols = orthonormal(image_cols)
    coefficients = basis_cols.astype(jnp.bfloat16)
    product = lax.dot_general(coefficients.astype(jnp.float32), stacked.astype(jnp.float32), (((0,), (0,)), ((), ())), preferred_element_type=jnp.float32)
    merged_piece = (product * (1.0 / math.sqrt(2 * SNAP))).astype(jnp.bfloat16)
    return merged_piece.reshape((RANK,) + lower_data.shape[1:])

def reference(snapshots, lat_taps, lon_taps):
    coarse = lax.map(partial(coarsen, lat_taps=lat_taps, lon_taps=lon_taps), snapshots)
    stride = 2 ** LEVEL
    results = {}
    pieces = []
    for block_index in range(TIME_BLOCKS):
        lower_block = block_index - block_index // stride % 2 * stride
        if lower_block not in results:
            results[lower_block] = merge_pair(coarse[lower_block], coarse[lower_block + stride])
        pieces.append(results[lower_block])
    return jnp.stack(pieces, axis=0)
```

```python
import functools
import math

import jax
import jax.numpy as jnp
from jax import lax
from jax.experimental import pallas as pl
from jax.experimental.pallas import tpu as pltpu
from jax.sharding import PartitionSpec as P

SNAP = 128
RANK = 128
VARS = 4
ITERS = 4
ROWS = 8
FINE_ROWS = 16
FINE = 256
CELLS = 1024
TAPS = 5
SPACE = 16

f32 = jnp.float32
bf16 = jnp.bfloat16
HIGHEST = lax.Precision.HIGHEST
MESH = pl.DeviceIdType.MESH


def dot(a, b, ca, cb, precision=None):
    return lax.dot_general(
        a, b, (((ca,), (cb,)), ((), ())), preferred_element_type=f32, precision=precision
    )


def lon_weights(taps, v, level):
    fine = lax.broadcasted_iota(jnp.int32, (FINE, FINE // 2), 0)
    coarse = lax.broadcasted_iota(jnp.int32, (FINE, FINE // 2), 1)
    offset = fine - 2 * coarse + TAPS // 2
    weights = jnp.zeros((FINE, FINE // 2), f32)
    for u in range(TAPS):
        weights = jnp.where(offset == u, taps[v, level, u], weights)
    high = weights.astype(bf16)
    low = (weights - high.astype(f32)).astype(bf16)
    return jnp.concatenate([high, low], axis=1)


def coarsen_block(fine, across, lat, lon, v, level, put):
    weights = lon_weights(lon, v, level)
    both = jnp.dot(
        fine[...].reshape(SNAP * FINE_ROWS, FINE), weights, preferred_element_type=f32
    )
    across[...] = both[:, : FINE // 2] + both[:, FINE // 2 :]
    rows = [across[pl.ds(k, SNAP, stride=FINE_ROWS), :] for k in range(FINE_ROWS)]
    for i in range(ROWS):
        total = None
        for a in range(TAPS):
            k = 2 * i + a - TAPS // 2
            if 0 <= k < FINE_ROWS:
                term = rows[k] * lat[v, level, a]
                total = term if total is None else total + term
        put(i, total.astype(bf16))


def wait_bytes(ref, sem):
    pltpu.make_async_copy(ref, ref, sem).wait()


def gram_kernel(
    x_hbm, lat, lon,
    kept, got, snd, gram,
    fine, across, own_src, own_rcv, own_all, cross_src, cross_rcv, cross_all,
    load_sem, chunk_send, chunk_recv, send_sem, recv_sem,
):
    tm = lax.axis_index("tm")
    sp = lax.axis_index("space")
    e = lax.rem(tm, 2)
    f = 1 - e
    pt = tm + 1 - 2 * e

    loads = []
    for c in range(2 * VARS):
        level = f if c < VARS else e
        load = pltpu.make_async_copy(x_hbm.at[0, :, c % VARS, level], fine.at[c], load_sem.at[c])
        load.start()
        loads.append(load)

    barrier = pltpu.get_barrier_semaphore()

    def greet(i, carry):
        s = lax.rem(sp + 1 + i, SPACE)
        pl.semaphore_signal(barrier, inc=1, device_id=(tm, s), device_id_type=MESH)
        return carry

    lax.fori_loop(0, SPACE - 1, greet, 0)

    def greet_partner(i, carry):
        pl.semaphore_signal(barrier, inc=1, device_id=(pt, i), device_id_type=MESH)
        return carry

    lax.fori_loop(0, SPACE, greet_partner, 0)

    copies = []
    for v in range(VARS):
        loads[v].wait()

        def put(i, value, v=v):
            snd[v, :, 128 * i : 128 * i + 128] = value

        coarsen_block(fine.at[v], across.at[v % 2], lat, lon, v, f, put)
        if v == 0:
            pl.semaphore_wait(barrier, 2 * SPACE - 1)
        copy = pltpu.make_async_remote_copy(
            src_ref=snd.at[v],
            dst_ref=got.at[v],
            send_sem=chunk_send.at[v],
            recv_sem=chunk_recv.at[v],
            device_id=(pt, sp),
            device_id_type=MESH,
        )
        copy.start()
        copies.append(copy)
    for v in range(VARS):
        loads[VARS + v].wait()

        def put_own(i, value, v=v):
            kept[v, :, 128 * i : 128 * i + 128] = value

        coarsen_block(fine.at[VARS + v], across.at[v % 2], lat, lon, v, e, put_own)

    own = None
    for v in range(VARS):
        for block in (snd[v], kept[v]):
            term = dot(block, block, 1, 1)
            own = term if own is None else own + term
    for b in range(SPACE):
        own_src[b] = own[8 * b : 8 * b + 8, :]

    def far_first(i):
        half = lax.div(i + 1, 2)
        return lax.rem(sp + SPACE // 2 + (1 - 2 * lax.rem(i, 2)) * half, SPACE)

    def scatter_own(i, carry):
        s = far_first(i)
        pltpu.make_async_remote_copy(
            src_ref=own_src.at[s],
            dst_ref=own_rcv.at[sp],
            send_sem=send_sem.at[0],
            recv_sem=recv_sem.at[0],
            device_id=(tm, s),
            device_id_type=MESH,
        ).start()
        return carry

    lax.fori_loop(0, SPACE - 1, scatter_own, 0)
    own_rcv[sp] = own_src[sp]
    wait_bytes(own_rcv.at[pl.ds(0, SPACE - 1)], recv_sem.at[0])
    total = own_rcv[0]
    for s in range(1, SPACE):
        total = total + own_rcv[s]
    mine = e * SPACE + sp
    own_all[mine] = total

    def gather_to(src, sem, partner):
        def body(i, carry):
            s = far_first(i)
            pltpu.make_async_remote_copy(
                src_ref=src,
                dst_ref=src,
                send_sem=send_sem.at[sem],
                recv_sem=recv_sem.at[sem],
                device_id=(pt if partner else tm, s),
                device_id_type=MESH,
            ).start()
            return carry

        lax.fori_loop(0, SPACE if partner else SPACE - 1, body, 0)

    gather_to(own_all.at[mine], 1, True)
    gather_to(own_all.at[mine], 1, False)

    cross = None
    for v in range(VARS):
        copies[v].wait_recv()
        term = dot(kept[v], got[v], 1, 1)
        cross = term if cross is None else cross + term
    cross = jnp.where(e == 0, cross, cross.T)
    for b in range(2 * SPACE):
        cross_src[b] = cross[4 * b : 4 * b + 4, :]
    slot = 2 * sp + e

    def scatter_cross(partner):
        def body(i, carry):
            s = far_first(i)
            pltpu.make_async_remote_copy(
                src_ref=cross_src.at[2 * s + (f if partner else e)],
                dst_ref=cross_rcv.at[slot],
                send_sem=send_sem.at[2],
                recv_sem=recv_sem.at[2],
                device_id=(pt if partner else tm, s),
                device_id_type=MESH,
            ).start()
            return carry

        lax.fori_loop(0, SPACE if partner else SPACE - 1, body, 0)

    scatter_cross(True)
    scatter_cross(False)
    cross_rcv[slot] = cross_src[slot]
    wait_bytes(cross_rcv.at[pl.ds(0, 2 * SPACE - 1)], recv_sem.at[2])
    total = cross_rcv[0]
    for s in range(1, 2 * SPACE):
        total = total + cross_rcv[s]
    cross_all[slot] = total
    gather_to(cross_all.at[slot], 3, True)
    gather_to(cross_all.at[slot], 3, False)

    wait_bytes(own_all.at[pl.ds(0, 2 * SPACE - 1)], recv_sem.at[1])
    for b in range(SPACE):
        gram[8 * b : 8 * b + 8, :SNAP] = own_all[b]
        gram[SNAP + 8 * b : SNAP + 8 * b + 8, SNAP:] = own_all[SPACE + b]
    wait_bytes(cross_all.at[pl.ds(0, 2 * SPACE - 1)], recv_sem.at[3])
    for b in range(2 * SPACE):
        gram[4 * b : 4 * b + 4, SNAP:] = cross_all[b]
    gram[SNAP:, :SNAP] = gram[:SNAP, SNAP:].T

    for v in range(VARS):
        copies[v].wait_send()
    wait_bytes(own_src.at[pl.ds(0, SPACE - 1)], send_sem.at[0])
    wait_bytes(own_all.at[pl.ds(0, 2 * SPACE - 1)], send_sem.at[1])
    wait_bytes(cross_src.at[pl.ds(0, 2 * SPACE - 1)], send_sem.at[2])
    wait_bytes(cross_all.at[pl.ds(0, 2 * SPACE - 1)], send_sem.at[3])


def pair_gram(snapshots, lat, lon):
    vmem = pltpu.VMEM
    return pl.pallas_call(
        gram_kernel,
        out_shape=(
            jax.ShapeDtypeStruct((VARS, SNAP, CELLS), bf16),
            jax.ShapeDtypeStruct((VARS, SNAP, CELLS), bf16),
            jax.ShapeDtypeStruct((VARS, SNAP, CELLS), bf16),
            jax.ShapeDtypeStruct((2 * SNAP, 2 * SNAP), f32),
        ),
        in_specs=[
            pl.BlockSpec(memory_space=pl.ANY),
            pl.BlockSpec(memory_space=pltpu.SMEM),
            pl.BlockSpec(memory_space=pltpu.SMEM),
        ],
        out_specs=(pl.BlockSpec(memory_space=vmem),) * 4,
        scratch_shapes=[
            vmem((2 * VARS, SNAP, FINE_ROWS, FINE), bf16),
            vmem((2, SNAP * FINE_ROWS, FINE // 2), f32),
            vmem((SPACE, 8, SNAP), f32),
            vmem((SPACE, 8, SNAP), f32),
            vmem((2 * SPACE, 8, SNAP), f32),
            vmem((2 * SPACE, 4, SNAP), f32),
            vmem((2 * SPACE, 4, SNAP), f32),
            vmem((2 * SPACE, 4, SNAP), f32),
            pltpu.SemaphoreType.DMA((2 * VARS,)),
            pltpu.SemaphoreType.DMA((VARS,)),
            pltpu.SemaphoreType.DMA((VARS,)),
            pltpu.SemaphoreType.DMA((4,)),
            pltpu.SemaphoreType.DMA((4,)),
        ],
        compiler_params=pltpu.CompilerParams(collective_id=0, has_side_effects=True),
        name="pair_gram",
    )(snapshots, lat, lon)


def lanes(x, k):
    return jnp.broadcast_to(x[:, k : k + 1], (8, RANK))


def sublanes(x, r):
    return jnp.broadcast_to(x[r : r + 1, :], (8, RANK))


def inverse_factor(product, eye):
    a = [product[8 * i : 8 * i + 8, :] for i in range(RANK // 8)]
    w = [eye[8 * i : 8 * i + 8, :] for i in range(RANK // 8)]
    sub = lax.broadcasted_iota(jnp.int32, (8, RANK), 0)
    out = []
    for j in range(RANK // 8):
        cols = [lanes(a[j], 8 * j + b) for b in range(8)]
        d = {(p, q): sublanes(cols[q], p) for q in range(8) for p in range(q + 1)}
        inv = []
        m = {}
        for k in range(8):
            inv.append(1.0 / d[k, k])
            for q in range(k + 1, 8):
                m[k, q] = d[k, q] * inv[k]
            for q in range(k + 1, 8):
                for p in range(k + 1, q + 1):
                    d[p, q] = d[p, q] - d[k, p] * m[k, q]
        rows_a, rows_w = [], []
        for q in range(8):
            ra, rw = sublanes(a[j], q), sublanes(w[j], q)
            for p in range(q):
                ra = ra - m[p, q] * rows_a[p]
                rw = rw - m[p, q] * rows_w[p]
            rows_a.append(ra)
            rows_w.append(rw)
        block = rows_w[0] * lax.rsqrt(d[0, 0])
        for q in range(1, 8):
            block = jnp.where(sub == q, rows_w[q] * lax.rsqrt(d[q, q]), block)
        out.append(block)
        for i in range(j + 1, RANK // 8):
            c = [lanes(a[i], 8 * j + b) for b in range(8)]
            for q in range(8):
                for p in range(q):
                    c[q] = c[q] - m[p, q] * c[p]
            for q in range(8):
                factor = c[q] * inv[q]
                a[i] = a[i] - factor * rows_a[q]
                w[i] = w[i] - factor * rows_w[q]
    return jnp.concatenate(out, axis=0)


def iterate_kernel(gram, coef):
    row = lax.broadcasted_iota(jnp.int32, (RANK, RANK), 0)
    col = lax.broadcasted_iota(jnp.int32, (RANK, RANK), 1)
    eye = (row == col).astype(f32)

    def orthonormal(image):
        product = dot(image, image, 1, 1, HIGHEST)
        return dot(inverse_factor(product, eye), image, 1, 0, HIGHEST)

    basis = orthonormal(gram[:RANK, :] + gram[RANK:, :])
    basis = lax.fori_loop(
        0, ITERS - 1, lambda _, b: orthonormal(dot(b, gram[...], 1, 0, HIGHEST)), basis
    )
    coef[...] = basis.astype(bf16)


def iterate(gram):
    return pl.pallas_call(
        iterate_kernel,
        out_shape=jax.ShapeDtypeStruct((RANK, 2 * SNAP), bf16),
        in_specs=[pl.BlockSpec(memory_space=pltpu.VMEM)],
        out_specs=pl.BlockSpec(memory_space=pltpu.VMEM),
        cost_estimate=pl.CostEstimate(flops=20_000_000_000, bytes_accessed=400_000, transcendentals=0),
        name="iterate",
    )(gram)


def merge_kernel(coef, kept, got, snd, rcv, out):
    e = lax.rem(lax.axis_index("tm"), 2)
    low, high = coef[:, :SNAP], coef[:, SNAP:]
    lower = e == 0
    own = jnp.where(lower, low, high)
    other = jnp.where(lower, high, low)
    row = lax.broadcasted_iota(jnp.int32, (2 * RANK, RANK), 0)
    col = lax.broadcasted_iota(jnp.int32, (2 * RANK, RANK), 1)

    def spread(level, value):
        return dot((row == 2 * col + level).astype(bf16), value, 1, 0).astype(bf16)

    left = jnp.concatenate(
        [spread(e, own), spread(e, other), spread(1 - e, own), spread(1 - e, other)], axis=1
    )
    for v in range(VARS):
        right = jnp.concatenate([kept[v], got[v], snd[v], rcv[v]], axis=0)
        product = dot(left, right, 1, 0) * (1.0 / math.sqrt(2 * SNAP))
        out[:, v] = product.astype(bf16).reshape(RANK, 2, CELLS)


def merge(coef, kept, got, snd, rcv):
    return pl.pallas_call(
        merge_kernel,
        out_shape=jax.ShapeDtypeStruct((RANK, VARS, 2, CELLS), bf16),
        in_specs=[pl.BlockSpec(memory_space=pltpu.VMEM)] * 5,
        out_specs=pl.BlockSpec(memory_space=pltpu.VMEM),
        name="merge",
    )(coef, kept, got, snd, rcv)


def local(snapshots, lat_taps, lon_taps):
    kept, got, snd, gram = pair_gram(snapshots, lat_taps, lon_taps)
    pairs = [(source, source ^ 1) for source in range(lax.axis_size("tm"))]
    rcv = lax.ppermute(kept, "tm", pairs)
    coef = iterate(gram)
    return merge(coef, kept, got, snd, rcv)[None]


def solution(mesh):
    return jax.shard_map(
        local,
        mesh=mesh,
        in_specs=(
            P("tm", None, None, "space", None, None),
            P(None, "space", None),
            P(None, "space", None),
        ),
        out_specs=P("tm", None, None, "space", None),
        check_vma=False,
    )
```

```python
import functools
import math

import jax
import jax.numpy as jnp
from jax import lax
from jax.experimental import pallas as pl
from jax.experimental.pallas import tpu as pltpu
from jax.sharding import PartitionSpec as P

SNAP = 128
RANK = 128
VARS = 4
ITERS = 4
ROWS = 8
FINE_ROWS = 16
FINE = 256
CELLS = 1024
TAPS = 5
SPACE = 16
EARLY = 1
AHEAD = 3

f32 = jnp.float32
bf16 = jnp.bfloat16
HIGHEST = lax.Precision.HIGHEST
MESH = pl.DeviceIdType.MESH


def dot(a, b, ca, cb, precision=None):
    return lax.dot_general(
        a, b, (((ca,), (cb,)), ((), ())), preferred_element_type=f32, precision=precision
    )


def lon_weights(taps, v, level):
    fine = lax.broadcasted_iota(jnp.int32, (FINE, FINE // 2), 0)
    coarse = lax.broadcasted_iota(jnp.int32, (FINE, FINE // 2), 1)
    offset = fine - 2 * coarse + TAPS // 2
    weights = jnp.zeros((FINE, FINE // 2), f32)
    for u in range(TAPS):
        weights = jnp.where(offset == u, taps[v, level, u], weights)
    high = weights.astype(bf16)
    low = (weights - high.astype(f32)).astype(bf16)
    return jnp.concatenate([high, low], axis=1)


def coarsen_block(fine, across, lat, lon, v, level, put):
    weights = lon_weights(lon, v, level)
    both = jnp.dot(
        fine[...].reshape(SNAP * FINE_ROWS, FINE), weights, preferred_element_type=f32
    )
    across[...] = both[:, : FINE // 2] + both[:, FINE // 2 :]
    rows = [across[pl.ds(k, SNAP, stride=FINE_ROWS), :] for k in range(FINE_ROWS)]
    for i in range(ROWS):
        total = None
        for a in range(TAPS):
            k = 2 * i + a - TAPS // 2
            if 0 <= k < FINE_ROWS:
                term = rows[k] * lat[v, level, a]
                total = term if total is None else total + term
        put(i, total.astype(bf16))


def wait_bytes(ref, sem):
    pltpu.make_async_copy(ref, ref, sem).wait()


def gram_kernel(
    x_hbm, lat_hbm, lon_hbm,
    early, late, got, snd, rest, gram,
    lat, lon, fine, across, own_src, own_rcv, own_all, cross_src, cross_rcv, cross_all,
    tap_sem, load_sem, chunk_send, chunk_recv, early_send, early_recv, send_sem, recv_sem,
):
    tm = lax.axis_index("tm")
    sp = lax.axis_index("space")
    e = lax.rem(tm, 2)
    f = 1 - e
    pt = tm + 1 - 2 * e

    def kept(v):
        return early.at[v] if v < EARLY else late.at[v - EARLY]

    taps = [
        pltpu.make_async_copy(lat_hbm, lat, tap_sem.at[0]),
        pltpu.make_async_copy(lon_hbm, lon, tap_sem.at[1]),
    ]
    for copy in taps:
        copy.start()
    loads = []
    for c in range(2 * VARS):
        level = f if c < VARS else e
        load = pltpu.make_async_copy(x_hbm.at[0, :, c % VARS, level], fine.at[c], load_sem.at[c])
        load.start()
        loads.append(load)

    barrier = pltpu.get_barrier_semaphore()

    def greet(i, carry):
        s = lax.rem(sp + 1 + i, SPACE)
        pl.semaphore_signal(barrier, inc=1, device_id=(tm, s), device_id_type=MESH)
        return carry

    lax.fori_loop(0, SPACE - 1, greet, 0)

    def greet_partner(i, carry):
        pl.semaphore_signal(barrier, inc=1, device_id=(pt, i), device_id_type=MESH)
        return carry

    lax.fori_loop(0, SPACE, greet_partner, 0)

    for copy in taps:
        copy.wait()
    copies = []
    for v in range(VARS):
        loads[v].wait()

        def put(i, value, v=v):
            snd[v, :, 128 * i : 128 * i + 128] = value

        coarsen_block(fine.at[v], across.at[v % 2], lat, lon, v, f, put)
        if v == 0:
            pl.semaphore_wait(barrier, 2 * SPACE - 1)
        copy = pltpu.make_async_remote_copy(
            src_ref=snd.at[v],
            dst_ref=got.at[v],
            send_sem=chunk_send.at[v],
            recv_sem=chunk_recv.at[v],
            device_id=(pt, sp),
            device_id_type=MESH,
        )
        copy.start()
        copies.append(copy)
    for v in range(VARS):
        loads[VARS + v].wait()

        def put_own(i, value, v=v):
            kept(v)[:, 128 * i : 128 * i + 128] = value

        coarsen_block(fine.at[VARS + v], across.at[v % 2], lat, lon, v, e, put_own)

    own = None
    for v in range(VARS):
        for block in (snd[v], kept(v)[...]):
            term = dot(block, block, 1, 1)
            own = term if own is None else own + term
    for b in range(SPACE):
        own_src[b] = own[8 * b : 8 * b + 8, :]

    def far_first(i):
        half = lax.div(i + 1, 2)
        return lax.rem(sp + SPACE // 2 + (1 - 2 * lax.rem(i, 2)) * half, SPACE)

    def scatter_own(i, carry):
        s = far_first(i)
        pltpu.make_async_remote_copy(
            src_ref=own_src.at[s],
            dst_ref=own_rcv.at[sp],
            send_sem=send_sem.at[0],
            recv_sem=recv_sem.at[0],
            device_id=(tm, s),
            device_id_type=MESH,
        ).start()
        return carry

    lax.fori_loop(0, SPACE - 1, scatter_own, 0)
    own_rcv[sp] = own_src[sp]
    wait_bytes(own_rcv.at[pl.ds(0, SPACE - 1)], recv_sem.at[0])
    total = own_rcv[0]
    for s in range(1, SPACE):
        total = total + own_rcv[s]
    mine = e * SPACE + sp
    own_all[mine] = total

    def gather_to(src, sem, partner):
        def body(i, carry):
            s = far_first(i)
            pltpu.make_async_remote_copy(
                src_ref=src,
                dst_ref=src,
                send_sem=send_sem.at[sem],
                recv_sem=recv_sem.at[sem],
                device_id=(pt if partner else tm, s),
                device_id_type=MESH,
            ).start()
            return carry

        lax.fori_loop(0, SPACE if partner else SPACE - 1, body, 0)

    gather_to(own_all.at[mine], 1, True)
    gather_to(own_all.at[mine], 1, False)

    cross = None
    for v in range(VARS):
        copies[v].wait_recv()
        term = dot(kept(v)[...], got[v], 1, 1)
        cross = term if cross is None else cross + term
    cross = jnp.where(e == 0, cross, cross.T)
    for b in range(2 * SPACE):
        cross_src[b] = cross[4 * b : 4 * b + 4, :]
    slot = 2 * sp + e

    def scatter_cross(partner):
        def body(i, carry):
            s = far_first(i)
            pltpu.make_async_remote_copy(
                src_ref=cross_src.at[2 * s + (f if partner else e)],
                dst_ref=cross_rcv.at[slot],
                send_sem=send_sem.at[2],
                recv_sem=recv_sem.at[2],
                device_id=(pt if partner else tm, s),
                device_id_type=MESH,
            ).start()
            return carry

        lax.fori_loop(0, SPACE if partner else SPACE - 1, body, 0)

    scatter_cross(True)
    scatter_cross(False)
    for v in range(EARLY):
        copy = pltpu.make_async_remote_copy(
            src_ref=early.at[v],
            dst_ref=rest.at[v],
            send_sem=early_send.at[v],
            recv_sem=early_recv.at[v],
            device_id=(pt, sp),
            device_id_type=MESH,
        )
        copy.start()
        copies.append(copy)
    cross_rcv[slot] = cross_src[slot]
    wait_bytes(cross_rcv.at[pl.ds(0, 2 * SPACE - 1)], recv_sem.at[2])
    total = cross_rcv[0]
    for s in range(1, 2 * SPACE):
        total = total + cross_rcv[s]
    cross_all[slot] = total
    gather_to(cross_all.at[slot], 3, True)
    gather_to(cross_all.at[slot], 3, False)

    wait_bytes(own_all.at[pl.ds(0, 2 * SPACE - 1)], recv_sem.at[1])
    for b in range(SPACE):
        gram[8 * b : 8 * b + 8, :SNAP] = own_all[b]
        gram[SNAP + 8 * b : SNAP + 8 * b + 8, SNAP:] = own_all[SPACE + b]
    wait_bytes(cross_all.at[pl.ds(0, 2 * SPACE - 1)], recv_sem.at[3])
    for b in range(2 * SPACE):
        gram[4 * b : 4 * b + 4, SNAP:] = cross_all[b]
    gram[SNAP:, :SNAP] = gram[:SNAP, SNAP:].T

    for copy in copies:
        copy.wait_send()
    for copy in copies[VARS:]:
        copy.wait_recv()
    wait_bytes(own_src.at[pl.ds(0, SPACE - 1)], send_sem.at[0])
    wait_bytes(own_all.at[pl.ds(0, 2 * SPACE - 1)], send_sem.at[1])
    wait_bytes(cross_src.at[pl.ds(0, 2 * SPACE - 1)], send_sem.at[2])
    wait_bytes(cross_all.at[pl.ds(0, 2 * SPACE - 1)], send_sem.at[3])


def pair_gram(snapshots, lat, lon):
    vmem = pltpu.VMEM
    return pl.pallas_call(
        gram_kernel,
        out_shape=(
            jax.ShapeDtypeStruct((EARLY, SNAP, CELLS), bf16),
            jax.ShapeDtypeStruct((VARS - EARLY, SNAP, CELLS), bf16),
            jax.ShapeDtypeStruct((VARS, SNAP, CELLS), bf16),
            jax.ShapeDtypeStruct((VARS, SNAP, CELLS), bf16),
            jax.ShapeDtypeStruct((EARLY, SNAP, CELLS), bf16),
            jax.ShapeDtypeStruct((2 * SNAP, 2 * SNAP), f32),
        ),
        in_specs=[
            pl.BlockSpec(memory_space=pltpu.HBM),
            pl.BlockSpec(memory_space=pltpu.HBM),
            pl.BlockSpec(memory_space=pltpu.HBM),
        ],
        out_specs=(pl.BlockSpec(memory_space=vmem),) * 6,
        scratch_shapes=[
            pltpu.SMEM((VARS, 2, TAPS), f32),
            pltpu.SMEM((VARS, 2, TAPS), f32),
            vmem((2 * VARS, SNAP, FINE_ROWS, FINE), bf16),
            vmem((2, SNAP * FINE_ROWS, FINE // 2), f32),
            vmem((SPACE, 8, SNAP), f32),
            vmem((SPACE, 8, SNAP), f32),
            vmem((2 * SPACE, 8, SNAP), f32),
            vmem((2 * SPACE, 4, SNAP), f32),
            vmem((2 * SPACE, 4, SNAP), f32),
            vmem((2 * SPACE, 4, SNAP), f32),
            pltpu.SemaphoreType.DMA((2,)),
            pltpu.SemaphoreType.DMA((2 * VARS,)),
            pltpu.SemaphoreType.DMA((VARS,)),
            pltpu.SemaphoreType.DMA((VARS,)),
            pltpu.SemaphoreType.DMA((EARLY,)),
            pltpu.SemaphoreType.DMA((EARLY,)),
            pltpu.SemaphoreType.DMA((4,)),
            pltpu.SemaphoreType.DMA((4,)),
        ],
        compiler_params=pltpu.CompilerParams(collective_id=0, has_side_effects=True, vmem_limit_bytes=48 << 20),
        name="pair_gram",
    )(snapshots, lat, lon)


def lanes(x, k):
    return jnp.broadcast_to(x[:, k : k + 1], (8, RANK))


def sublanes(x, r):
    return jnp.broadcast_to(x[r : r + 1, :], (8, RANK))


def split3(x):
    high = x.astype(bf16)
    left = x - high.astype(f32)
    middle = left.astype(bf16)
    return high, middle, (left - middle.astype(f32)).astype(bf16)


def tree_sum(terms):
    while len(terms) > 1:
        terms = [x + y for x, y in zip(terms[::2], terms[1::2])]
    return terms[0]


def inverse_factor(product, eye):
    blocks = RANK // 8
    a = [product[8 * i : 8 * i + 8, :] for i in range(blocks)]
    w = [eye[8 * i : 8 * i + 8, :] for i in range(blocks)]
    sub = lax.broadcasted_iota(jnp.int32, (8, RANK), 0)
    out = []
    for j in range(blocks):
        last = j == blocks - 1
        cols = [lanes(a[j], 8 * j + b) for b in range(8)]
        d = {(p, q): sublanes(cols[q], p) for q in range(8) for p in range(q + 1)}
        rows_a = [sublanes(a[j], q) for q in range(8)]
        rows_w = [sublanes(w[j], q) for q in range(8)]
        inv = []
        m = {}
        for k in range(8):
            inv.append(1.0 / d[k, k])
            for q in range(k + 1, 8):
                m[k, q] = d[k, q] * inv[k]
            for q in range(k + 1, 8):
                for p in range(k + 1, q + 1):
                    d[p, q] = d[p, q] - d[k, p] * m[k, q]
                if not last:
                    rows_a[q] = rows_a[q] - m[k, q] * rows_a[k]
                rows_w[q] = rows_w[q] - m[k, q] * rows_w[k]
        root = [lax.rsqrt(d[q, q]) for q in range(8)]

        def pick(rows):
            block = rows[0] * root[0]
            for q in range(1, 8):
                block = jnp.where(sub == q, rows[q] * root[q], block)
            return block

        block_w = pick(rows_w)
        out.append(block_w)
        if last:
            break
        far = j + AHEAD + 1
        if far < blocks:
            ah, am, al = split3(pick(rows_a))
            wh, wm, wl = split3(block_w)
            right = jnp.concatenate(
                [
                    jnp.concatenate(pair, axis=1)
                    for pair in ((ah, wh), (am, wm), (ah, wh), (am, wm), (al, wl), (ah, wh))
                ],
                axis=0,
            )
            left = jnp.concatenate([ah, ah, am, am, ah, al], axis=0)[:, 8 * far :]
            update = dot(left, right, 0, 0)
        for i in range(j + 1, min(far, blocks)):
            c = [lanes(a[i], 8 * j + q) for q in range(8)]
            for q in range(8):
                for p in range(q):
                    c[q] = c[q] - m[p, q] * c[p]
            factor = [c[q] * inv[q] for q in range(8)]
            a[i] = a[i] - tree_sum([factor[q] * rows_a[q] for q in range(8)])
            w[i] = w[i] - tree_sum([factor[q] * rows_w[q] for q in range(8)])
        for i in range(far, blocks):
            r = 8 * (i - far)
            a[i] = a[i] - update[r : r + 8, :RANK]
            w[i] = w[i] - update[r : r + 8, RANK:]
    return jnp.concatenate(out, axis=0)


def iterate_kernel(gram, coef):
    row = lax.broadcasted_iota(jnp.int32, (RANK, RANK), 0)
    col = lax.broadcasted_iota(jnp.int32, (RANK, RANK), 1)
    eye = (row == col).astype(f32)

    def orthonormal(image):
        product = dot(image, image, 1, 1, HIGHEST)
        return dot(inverse_factor(product, eye), image, 1, 0, HIGHEST)

    basis = orthonormal(gram[:RANK, :] + gram[RANK:, :])
    basis = lax.fori_loop(
        0, ITERS - 1, lambda _, b: orthonormal(dot(b, gram[...], 1, 0, HIGHEST)), basis
    )
    coef[...] = basis.astype(bf16)


def iterate(gram):
    return pl.pallas_call(
        iterate_kernel,
        out_shape=jax.ShapeDtypeStruct((RANK, 2 * SNAP), bf16),
        in_specs=[pl.BlockSpec(memory_space=pltpu.VMEM)],
        out_specs=pl.BlockSpec(memory_space=pltpu.VMEM),
        cost_estimate=pl.CostEstimate(flops=20_000_000_000, bytes_accessed=400_000, transcendentals=0),
        compiler_params=pltpu.CompilerParams(vmem_limit_bytes=8 << 20),
        name="iterate",
    )(gram)


def merge_kernel(coef, early, late, got, snd, rest, rcv, out, left):
    v = pl.program_id(0)

    @pl.when(v == 0)
    def _():
        e = lax.rem(lax.axis_index("tm"), 2)
        low, high = coef[:, :SNAP], coef[:, SNAP:]
        own = jnp.where(e == 0, low, high)
        other = jnp.where(e == 0, high, low)
        row = lax.broadcasted_iota(jnp.int32, (2 * RANK, RANK), 0)
        col = lax.broadcasted_iota(jnp.int32, (2 * RANK, RANK), 1)
        for k, (level, value) in enumerate(((e, own), (e, other), (1 - e, own), (1 - e, other))):
            spread = dot((row == 2 * col + level).astype(bf16), value, 1, 0)
            left[:, SNAP * k : SNAP * k + SNAP] = spread.astype(bf16)

    def put(kept, received):
        right = jnp.concatenate([kept[0], got[0], snd[0], received[0]], axis=0)
        product = dot(left[...], right, 1, 0) * (1.0 / math.sqrt(2 * SNAP))
        out[:, 0] = product.astype(bf16).reshape(RANK, 2, CELLS)

    @pl.when(v < EARLY)
    def _():
        put(early, rest)

    @pl.when(v >= EARLY)
    def _():
        put(late, rcv)


def merge(coef, early, late, got, snd, rest, rcv):
    first = pl.BlockSpec((1, SNAP, CELLS), lambda v: (jnp.minimum(v, EARLY - 1), 0, 0))
    second = pl.BlockSpec((1, SNAP, CELLS), lambda v: (jnp.maximum(v - EARLY, 0), 0, 0))
    every = pl.BlockSpec((1, SNAP, CELLS), lambda v: (v, 0, 0))
    return pl.pallas_call(
        merge_kernel,
        grid=(VARS,),
        out_shape=jax.ShapeDtypeStruct((RANK, VARS, 2, CELLS), bf16),
        in_specs=[
            pl.BlockSpec((RANK, 2 * SNAP), lambda v: (0, 0)),
            first, second, every, every, first, second,
        ],
        out_specs=pl.BlockSpec((RANK, 1, 2, CELLS), lambda v: (0, v, 0, 0)),
        scratch_shapes=[pltpu.VMEM((2 * RANK, 4 * SNAP), bf16)],
        compiler_params=pltpu.CompilerParams(vmem_limit_bytes=16 << 20),
        name="merge",
    )(coef, early, late, got, snd, rest, rcv)


def local(snapshots, lat_taps, lon_taps):
    lat_taps, lon_taps = (pltpu.with_memory_space_constraint(t, pltpu.HBM) for t in (lat_taps, lon_taps))
    early, late, got, snd, rest, gram = pair_gram(snapshots, lat_taps, lon_taps)
    pairs = [(source, source ^ 1) for source in range(lax.axis_size("tm"))]
    rcv = lax.ppermute(late, "tm", pairs)
    coef = iterate(gram)
    return merge(coef, early, late, got, snd, rest, rcv)[None]


def solution(mesh):
    return jax.shard_map(
        local,
        mesh=mesh,
        in_specs=(
            P("tm", None, None, "space", None, None),
            P(None, "space", None),
            P(None, "space", None),
        ),
        out_specs=P("tm", None, None, "space", None),
        check_vma=False,
    )
```

```python
import functools
import math

import jax
import jax.numpy as jnp
from jax import lax
from jax.experimental import pallas as pl
from jax.experimental.pallas import tpu as pltpu
from jax.sharding import PartitionSpec as P

SNAP = 128
RANK = 128
VARS = 4
ITERS = 4
ROWS = 8
FINE_ROWS = 16
FINE = 256
CELLS = 1024
TAPS = 5
SPACE = 16
HEAD = 40
AHEAD = 3

f32 = jnp.float32
bf16 = jnp.bfloat16
HIGHEST = lax.Precision.HIGHEST
MESH = pl.DeviceIdType.MESH


def dot(a, b, ca, cb, precision=None):
    return lax.dot_general(
        a, b, (((ca,), (cb,)), ((), ())), preferred_element_type=f32, precision=precision
    )


def lon_weights(taps, v, level):
    fine = lax.broadcasted_iota(jnp.int32, (FINE, FINE // 2), 0)
    coarse = lax.broadcasted_iota(jnp.int32, (FINE, FINE // 2), 1)
    offset = fine - 2 * coarse + TAPS // 2
    weights = jnp.zeros((FINE, FINE // 2), f32)
    for u in range(TAPS):
        weights = jnp.where(offset == u, taps[v, level, u], weights)
    high = weights.astype(bf16)
    low = (weights - high.astype(f32)).astype(bf16)
    return jnp.concatenate([high, low], axis=1)


def coarsen_block(fine, across, lat, lon, v, level, put):
    weights = lon_weights(lon, v, level)
    both = jnp.dot(
        fine[...].reshape(SNAP * FINE_ROWS, FINE), weights, preferred_element_type=f32
    )
    across[...] = both[:, : FINE // 2] + both[:, FINE // 2 :]
    rows = [across[pl.ds(k, SNAP, stride=FINE_ROWS), :] for k in range(FINE_ROWS)]
    for i in range(ROWS):
        total = None
        for a in range(TAPS):
            k = 2 * i + a - TAPS // 2
            if 0 <= k < FINE_ROWS:
                term = rows[k] * lat[v, level, a]
                total = term if total is None else total + term
        put(i, total.astype(bf16))


def wait_bytes(ref, sem):
    pltpu.make_async_copy(ref, ref, sem).wait()


def gram_kernel(
    x_hbm, lat_hbm, lon_hbm,
    early, late, got, snd, rest, gram,
    lat, lon, fine, across, own_src, own_rcv, own_all, cross_src, cross_rcv, cross_all,
    tap_sem, load_sem, chunk_send, chunk_recv, early_send, early_recv, pair_sem, send_sem, recv_sem,
):
    tm = lax.axis_index("tm")
    sp = lax.axis_index("space")
    e = lax.rem(tm, 2)
    f = 1 - e
    pt = tm + 1 - 2 * e

    def kept(v):
        return jnp.concatenate([early[v], late[v]], axis=0)

    taps = [
        pltpu.make_async_copy(lat_hbm, lat, tap_sem.at[0]),
        pltpu.make_async_copy(lon_hbm, lon, tap_sem.at[1]),
    ]
    for copy in taps:
        copy.start()
    loads = []
    for c in range(2 * VARS):
        level = f if c < VARS else e
        load = pltpu.make_async_copy(x_hbm.at[0, :, c % VARS, level], fine.at[c], load_sem.at[c])
        loads.append(load)
    loads[0].start()
    loads[1].start()

    barrier = pltpu.get_barrier_semaphore()

    def far_first(i):
        half = lax.div(i + 1, 2)
        return lax.rem(sp + SPACE // 2 + (1 - 2 * lax.rem(i, 2)) * half, SPACE)

    def greet(i, carry):
        s = far_first(i)
        pl.semaphore_signal(barrier, inc=1, device_id=(tm, s), device_id_type=MESH)
        return carry

    def greet_partner(i, carry):
        s = far_first(i)
        pl.semaphore_signal(barrier, inc=1, device_id=(pt, s), device_id_type=MESH)
        return carry

    lax.fori_loop(0, SPACE, greet_partner, 0)
    lax.fori_loop(0, SPACE - 1, greet, 0)

    for copy in taps:
        copy.wait()
    copies = []
    for v in range(VARS):
        loads[v].wait()
        loads[v + 2].start()

        def put(i, value, v=v):
            snd[v, :, 128 * i : 128 * i + 128] = value

        coarsen_block(fine.at[v], across.at[v % 2], lat, lon, v, f, put)
        copy = pltpu.make_async_remote_copy(
            src_ref=snd.at[v],
            dst_ref=got.at[v],
            send_sem=chunk_send.at[v],
            recv_sem=chunk_recv.at[v],
            device_id=(pt, sp),
            device_id_type=MESH,
        )
        copies.append(copy)
        if v == 1:
            pl.semaphore_wait(barrier, 2 * SPACE - 1)
            copies[0].start()
        if v >= 1:
            copy.start()
    for v in range(VARS):
        loads[VARS + v].wait()
        if v + 2 < VARS:
            loads[VARS + v + 2].start()

        def put_own(i, value, v=v):
            early[v, :, 128 * i : 128 * i + 128] = value[:HEAD]
            late[v, :, 128 * i : 128 * i + 128] = value[HEAD:]

        coarsen_block(fine.at[VARS + v], across.at[v % 2], lat, lon, v, e, put_own)

    own = None
    for v in range(VARS):
        for block in (snd[v], kept(v)):
            term = dot(block, block, 1, 1)
            own = term if own is None else own + term
    for b in range(SPACE):
        own_src[b] = own[8 * b : 8 * b + 8, :]

    def scatter_own(i, carry):
        s = far_first(i)
        pltpu.make_async_remote_copy(
            src_ref=own_src.at[s],
            dst_ref=own_rcv.at[sp],
            send_sem=send_sem.at[0],
            recv_sem=recv_sem.at[0],
            device_id=(tm, s),
            device_id_type=MESH,
        ).start()
        return carry

    lax.fori_loop(0, SPACE - 1, scatter_own, 0)
    own_rcv[sp] = own_src[sp]
    wait_bytes(own_rcv.at[pl.ds(0, SPACE - 1)], recv_sem.at[0])
    total = own_rcv[0]
    for s in range(1, SPACE):
        total = total + own_rcv[s]
    mine = e * SPACE + sp
    own_all[mine] = total

    def gather_to(src, sem, partner):
        def body(i, carry):
            s = far_first(i)
            pltpu.make_async_remote_copy(
                src_ref=src,
                dst_ref=src,
                send_sem=send_sem.at[sem],
                recv_sem=recv_sem.at[sem],
                device_id=(pt if partner else tm, s),
                device_id_type=MESH,
            ).start()
            return carry

        lax.fori_loop(0, SPACE if partner else SPACE - 1, body, 0)

    pair_copy = pltpu.make_async_remote_copy(
        src_ref=own_all.at[mine],
        dst_ref=own_all.at[mine],
        send_sem=pair_sem.at[0],
        recv_sem=pair_sem.at[1],
        device_id=(pt, sp),
        device_id_type=MESH,
    )
    pair_copy.start()
    gather_to(own_all.at[mine], 1, False)

    cross = None
    for v in range(VARS):
        copies[v].wait_recv()
        term = dot(kept(v), got[v], 1, 1)
        cross = term if cross is None else cross + term
    cross = jnp.where(e == 0, cross, cross.T)
    for b in range(2 * SPACE):
        cross_src[b] = cross[4 * b : 4 * b + 4, :]
    slot = 2 * sp + e

    def scatter_cross(partner):
        def body(i, carry):
            s = far_first(i)
            pltpu.make_async_remote_copy(
                src_ref=cross_src.at[2 * s + (f if partner else e)],
                dst_ref=cross_rcv.at[slot],
                send_sem=send_sem.at[2],
                recv_sem=recv_sem.at[2],
                device_id=(pt if partner else tm, s),
                device_id_type=MESH,
            ).start()
            return carry

        lax.fori_loop(0, SPACE if partner else SPACE - 1, body, 0)

    scatter_cross(True)
    scatter_cross(False)
    for v in range(VARS):
        copy = pltpu.make_async_remote_copy(
            src_ref=early.at[v],
            dst_ref=rest.at[v],
            send_sem=early_send.at[v],
            recv_sem=early_recv.at[v],
            device_id=(pt, sp),
            device_id_type=MESH,
        )
        copies.append(copy)
    for copy in copies[VARS:-1]:
        copy.start()
    pair_copy.wait_recv()
    gather_to(own_all.at[f * SPACE + sp], 1, False)
    cross_rcv[slot] = cross_src[slot]
    wait_bytes(cross_rcv.at[pl.ds(0, 2 * SPACE - 1)], recv_sem.at[2])
    total = cross_rcv[0]
    for s in range(1, 2 * SPACE):
        total = total + cross_rcv[s]
    cross_all[slot] = total
    gather_to(cross_all.at[slot], 3, True)
    gather_to(cross_all.at[slot], 3, False)
    copies[-1].start()

    wait_bytes(own_all.at[pl.ds(0, 2 * SPACE - 2)], recv_sem.at[1])
    for b in range(SPACE):
        gram[8 * b : 8 * b + 8, :SNAP] = own_all[b]
        gram[SNAP + 8 * b : SNAP + 8 * b + 8, SNAP:] = own_all[SPACE + b]
    wait_bytes(cross_all.at[pl.ds(0, 2 * SPACE - 1)], recv_sem.at[3])
    for b in range(2 * SPACE):
        gram[4 * b : 4 * b + 4, SNAP:] = cross_all[b]
    gram[SNAP:, :SNAP] = gram[:SNAP, SNAP:].T

    for copy in copies:
        copy.wait_send()
    for copy in copies[VARS:]:
        copy.wait_recv()
    wait_bytes(own_src.at[pl.ds(0, SPACE - 1)], send_sem.at[0])
    wait_bytes(own_all.at[pl.ds(0, 2 * SPACE - 2)], send_sem.at[1])
    pair_copy.wait_send()
    wait_bytes(cross_src.at[pl.ds(0, 2 * SPACE - 1)], send_sem.at[2])
    wait_bytes(cross_all.at[pl.ds(0, 2 * SPACE - 1)], send_sem.at[3])


def pair_gram(snapshots, lat, lon):
    vmem = pltpu.VMEM
    return pl.pallas_call(
        gram_kernel,
        out_shape=(
            jax.ShapeDtypeStruct((VARS, HEAD, CELLS), bf16),
            jax.ShapeDtypeStruct((VARS, SNAP - HEAD, CELLS), bf16),
            jax.ShapeDtypeStruct((VARS, SNAP, CELLS), bf16),
            jax.ShapeDtypeStruct((VARS, SNAP, CELLS), bf16),
            jax.ShapeDtypeStruct((VARS, HEAD, CELLS), bf16),
            jax.ShapeDtypeStruct((2 * SNAP, 2 * SNAP), f32),
        ),
        in_specs=[
            pl.BlockSpec(memory_space=pltpu.HBM),
            pl.BlockSpec(memory_space=pltpu.HBM),
            pl.BlockSpec(memory_space=pltpu.HBM),
        ],
        out_specs=(pl.BlockSpec(memory_space=vmem),) * 6,
        scratch_shapes=[
            pltpu.SMEM((VARS, 2, TAPS), f32),
            pltpu.SMEM((VARS, 2, TAPS), f32),
            vmem((2 * VARS, SNAP, FINE_ROWS, FINE), bf16),
            vmem((2, SNAP * FINE_ROWS, FINE // 2), f32),
            vmem((SPACE, 8, SNAP), f32),
            vmem((SPACE, 8, SNAP), f32),
            vmem((2 * SPACE, 8, SNAP), f32),
            vmem((2 * SPACE, 4, SNAP), f32),
            vmem((2 * SPACE, 4, SNAP), f32),
            vmem((2 * SPACE, 4, SNAP), f32),
            pltpu.SemaphoreType.DMA((2,)),
            pltpu.SemaphoreType.DMA((2 * VARS,)),
            pltpu.SemaphoreType.DMA((VARS,)),
            pltpu.SemaphoreType.DMA((VARS,)),
            pltpu.SemaphoreType.DMA((VARS,)),
            pltpu.SemaphoreType.DMA((VARS,)),
            pltpu.SemaphoreType.DMA((2,)),
            pltpu.SemaphoreType.DMA((4,)),
            pltpu.SemaphoreType.DMA((4,)),
        ],
        compiler_params=pltpu.CompilerParams(collective_id=0, has_side_effects=True, vmem_limit_bytes=48 << 20),
        name="pair_gram",
    )(snapshots, lat, lon)


def lanes(x, k):
    return jnp.broadcast_to(x[:, k : k + 1], (8, RANK))


def sublanes(x, r):
    return jnp.broadcast_to(x[r : r + 1, :], (8, RANK))


def split3(x):
    high = x.astype(bf16)
    left = x - high.astype(f32)
    middle = left.astype(bf16)
    return high, middle, (left - middle.astype(f32)).astype(bf16)


def tree_sum(terms):
    while len(terms) > 1:
        terms = [x + y for x, y in zip(terms[::2], terms[1::2])]
    return terms[0]


def inverse_factor(product, eye):
    blocks = RANK // 8
    a = [product[8 * i : 8 * i + 8, :] for i in range(blocks)]
    w = [eye[8 * i : 8 * i + 8, :] for i in range(blocks)]
    sub = lax.broadcasted_iota(jnp.int32, (8, RANK), 0)
    out = []
    for j in range(blocks):
        last = j == blocks - 1
        cols = [lanes(a[j], 8 * j + b) for b in range(8)]
        d = {(p, q): sublanes(cols[q], p) for q in range(8) for p in range(q + 1)}
        rows_a = [sublanes(a[j], q) for q in range(8)]
        rows_w = [sublanes(w[j], q) for q in range(8)]
        inv = []
        m = {}
        for k in range(8):
            inv.append(1.0 / d[k, k])
            for q in range(k + 1, 8):
                m[k, q] = d[k, q] * inv[k]
            for q in range(k + 1, 8):
                for p in range(k + 1, q + 1):
                    d[p, q] = d[p, q] - d[k, p] * m[k, q]
                if not last:
                    rows_a[q] = rows_a[q] - m[k, q] * rows_a[k]
                rows_w[q] = rows_w[q] - m[k, q] * rows_w[k]
        root = [lax.rsqrt(d[q, q]) for q in range(8)]

        def pick(rows):
            block = rows[0] * root[0]
            for q in range(1, 8):
                block = jnp.where(sub == q, rows[q] * root[q], block)
            return block

        block_w = pick(rows_w)
        out.append(block_w)
        if last:
            break
        far = j + AHEAD + 1
        if far < blocks:
            ah, am, al = split3(pick(rows_a))
            wh, wm, wl = split3(block_w)
            right = jnp.concatenate(
                [
                    jnp.concatenate(pair, axis=1)
                    for pair in ((ah, wh), (am, wm), (ah, wh), (am, wm), (al, wl), (ah, wh))
                ],
                axis=0,
            )
            left = jnp.concatenate([ah, ah, am, am, ah, al], axis=0)[:, 8 * far :]
            update = dot(left, right, 0, 0)
        for i in range(j + 1, min(far, blocks)):
            c = [lanes(a[i], 8 * j + q) for q in range(8)]
            for q in range(8):
                for p in range(q):
                    c[q] = c[q] - m[p, q] * c[p]
            factor = [c[q] * inv[q] for q in range(8)]
            a[i] = a[i] - tree_sum([factor[q] * rows_a[q] for q in range(8)])
            w[i] = w[i] - tree_sum([factor[q] * rows_w[q] for q in range(8)])
        for i in range(far, blocks):
            r = 8 * (i - far)
            a[i] = a[i] - update[r : r + 8, :RANK]
            w[i] = w[i] - update[r : r + 8, RANK:]
    return jnp.concatenate(out, axis=0)


def spread_left(parts):
    high, middle, low = parts
    return jnp.concatenate([high, high, middle, middle, high, low], axis=1)


def spread_right(parts):
    high, middle, low = parts
    return jnp.concatenate([high, middle, high, middle, low, high], axis=0)


def iterate_kernel(gram, coef, gram_parts):
    row = lax.broadcasted_iota(jnp.int32, (RANK, RANK), 0)
    col = lax.broadcasted_iota(jnp.int32, (RANK, RANK), 1)
    eye = (row == col).astype(f32)
    gram_parts[...] = spread_right(split3(gram[...]))

    def orthonormal(image):
        product = dot(image, image, 1, 1, HIGHEST)
        inverse = inverse_factor(product, eye)
        return dot(spread_left(split3(inverse)), spread_right(split3(image)), 1, 0)

    basis = orthonormal(gram[:RANK, :] + gram[RANK:, :])
    basis = lax.fori_loop(
        0,
        ITERS - 1,
        lambda _, b: orthonormal(dot(spread_left(split3(b)), gram_parts[...], 1, 0)),
        basis,
    )
    coef[...] = basis.astype(bf16)


def iterate(gram):
    return pl.pallas_call(
        iterate_kernel,
        out_shape=jax.ShapeDtypeStruct((RANK, 2 * SNAP), bf16),
        in_specs=[pl.BlockSpec(memory_space=pltpu.VMEM)],
        out_specs=pl.BlockSpec(memory_space=pltpu.VMEM),
        cost_estimate=pl.CostEstimate(flops=20_000_000_000, bytes_accessed=400_000, transcendentals=0),
        scratch_shapes=[pltpu.VMEM((12 * SNAP, 2 * SNAP), bf16)],
        compiler_params=pltpu.CompilerParams(vmem_limit_bytes=8 << 20),
        name="iterate",
    )(gram)


def merge_kernel(coef, early, late, got, snd, rest, rcv, out, left):
    v = pl.program_id(0)

    @pl.when(v == 0)
    def _():
        e = lax.rem(lax.axis_index("tm"), 2)
        low, high = coef[:, :SNAP], coef[:, SNAP:]
        own = jnp.where(e == 0, low, high)
        other = jnp.where(e == 0, high, low)
        row = lax.broadcasted_iota(jnp.int32, (2 * RANK, RANK), 0)
        col = lax.broadcasted_iota(jnp.int32, (2 * RANK, RANK), 1)
        for k, (level, value) in enumerate(((e, own), (e, other), (1 - e, own), (1 - e, other))):
            spread = dot((row == 2 * col + level).astype(bf16), value, 1, 0)
            left[:, SNAP * k : SNAP * k + SNAP] = spread.astype(bf16)

    right = jnp.concatenate([early[0], late[0], got[0], snd[0], rest[0], rcv[0]], axis=0)
    product = dot(left[...], right, 1, 0) * (1.0 / math.sqrt(2 * SNAP))
    out[:, 0] = product.astype(bf16).reshape(RANK, 2, CELLS)


def merge(coef, early, late, got, snd, rest, rcv):
    head = pl.BlockSpec((1, HEAD, CELLS), lambda v: (v, 0, 0))
    tail = pl.BlockSpec((1, SNAP - HEAD, CELLS), lambda v: (v, 0, 0))
    every = pl.BlockSpec((1, SNAP, CELLS), lambda v: (v, 0, 0))
    return pl.pallas_call(
        merge_kernel,
        grid=(VARS,),
        out_shape=jax.ShapeDtypeStruct((RANK, VARS, 2, CELLS), bf16),
        in_specs=[
            pl.BlockSpec((RANK, 2 * SNAP), lambda v: (0, 0)),
            head, tail, every, every, head, tail,
        ],
        out_specs=pl.BlockSpec((RANK, 1, 2, CELLS), lambda v: (0, v, 0, 0)),
        scratch_shapes=[pltpu.VMEM((2 * RANK, 4 * SNAP), bf16)],
        compiler_params=pltpu.CompilerParams(vmem_limit_bytes=16 << 20),
        name="merge",
    )(coef, early, late, got, snd, rest, rcv)


def local(snapshots, lat_taps, lon_taps):
    lat_taps, lon_taps = (pltpu.with_memory_space_constraint(t, pltpu.HBM) for t in (lat_taps, lon_taps))
    early, late, got, snd, rest, gram = pair_gram(snapshots, lat_taps, lon_taps)
    pairs = [(source, source ^ 1) for source in range(lax.axis_size("tm"))]
    rcv = lax.ppermute(late, "tm", pairs)
    coef = iterate(gram)
    return merge(coef, early, late, got, snd, rest, rcv)[None]


def solution(mesh):
    return jax.shard_map(
        local,
        mesh=mesh,
        in_specs=(
            P("tm", None, None, "space", None, None),
            P(None, "space", None),
            P(None, "space", None),
        ),
        out_specs=P("tm", None, None, "space", None),
        check_vma=False,
    )
```
